1024 devices in a mesh: tok: 32 (over x_lo, z), feat: 32 (over y, x_hi, core).
Axes of the slice: x: 4 (x_hi: 2, x_lo: 2; x = x_hi * 2 + x_lo), y: 8, z: 16, core: 2. Of those that a mesh axis runs over, the one named last changes fastest.
Arguments:
- patches: bfloat16 [384, 6144], P('tok', 'feat'), may hold values from -640 to 640
- frame_counts: int32 [32], P('tok'), may hold values from 1 to 3
- patch_mask: int32 [384], P('tok'), may hold values 0 or 1
- norm_gain: float32 [6144], P('feat'), may hold values from 0.1 to 1.9
- up_weight: bfloat16 [6144, 24576], P('feat', 'tok'), may hold values from -0.078125 to 0.078125
- up_bias: float32 [24576], P('tok'), may hold values from -3 to 3
- down_weight: bfloat16 [24576, 6144], P('tok', 'feat'), may hold values from -0.0390625 to 0.0390625
- down_bias: float32 [6144], P('feat'), may hold values from -3 to 3
Outputs:
- block_output: bfloat16 [384, 6144], P('tok', 'feat')
The draws below stay inside these ranges and needn't reach their ends.
All inputs are finite; a program needn't handle non-finite values. No bound on the sum of `patch_mask` on one device may be relied on, other than what follows from the above.
Results may differ from the reference program's by a relative error of at most 0.0053.
Values may be sent and summed in bfloat16 or wider, within the bound.
A program may use at most 32 MiB of HBM per device.

```python
import jax
import jax.numpy as jnp
from jax import lax

D = 6144
FF = 24576
FRAME_TOK = 4
FRAMES = 3
TOK_DEV = 12
CLIPS = 32
TOKENS = 384


def draw_patches(key, part):
    first_key, second_key = jax.random.split(key, 2)
    column = jnp.arange(D, dtype=jnp.float32) / D
    row_scale = 10.0 ** jax.random.uniform(second_key, (TOKENS, 1), dtype=jnp.float32)
    base = jax.random.normal(first_key, (TOKENS, D), dtype=jnp.float32)
    col_scale = 10.0 ** column
    return (base * col_scale[None, :] * row_scale).astype(jnp.bfloat16)


def plant(entries, own_key, smallest, high):
    index_at = [jax.random.randint(jax.random.fold_in(own_key, axis), (), 0, length) for axis, length in enumerate(entries.shape)]
    widest = entries.shape.index(max(entries.shape))
    next_to = index_at[:widest] + [(index_at[widest] + 1) % entries.shape[widest]] + index_at[widest + 1:]
    return entries.at[tuple(index_at)].set(smallest).at[tuple(next_to)].set(high)


def block_levels(rng, shape, pieces, smallest, top_value):
    def one(axis_at, parts):
        draws = jax.random.uniform(jax.random.fold_in(jax.random.fold_in(rng, 6), axis_at), (parts,), jnp.float32, smallest / len(pieces), top_value / len(pieces))
        return jnp.repeat(jnp.exp(draws), shape[axis_at] // parts).reshape((-1,) + (1,) * (len(shape) - axis_at - 1))

    loudness = one(*pieces[0])
    for cut in pieces[1:]:
        loudness = loudness * one(*cut)
    return loudness


def normal_values(rng, dims, deviation, reach, pieces=(), kind=jnp.bfloat16):
    values = jax.random.normal(rng, dims, jnp.float32) * deviation
    if len(pieces) > 0:
        values = block_levels(rng, dims, pieces, -0.22, 0.18) * values
    return jnp.clip(values, min=-reach, max=reach).astype(kind)


def setup_inputs(seed: int = 0) -> dict:
    key_of = jax.random.split(jax.random.key(seed), 9)
    patches = draw_patches(jax.random.fold_in(key_of[8], 71), 0)
    frame_counts = plant(jax.random.randint(key_of[1], (CLIPS,), 1, FRAMES + 1), jax.random.fold_in(key_of[1], 1), 1, FRAMES).astype(jnp.int32)
    patch_mask = plant((jax.random.randint(key_of[2], (TOKENS,), 0, 8) < 7).astype(jnp.int32), jax.random.fold_in(key_of[2], 1), 0, 1)
    norm_gain = jnp.clip(1.0 + 0.18 * jax.random.normal(key_of[3], (D,), jnp.float32), 0.1, 1.9)
    up_weight = normal_values(key_of[4], (D, FF), D ** -0.5, 0.078125, ((0, 32), (1, 32)))
    up_bias = normal_values(key_of[5], (FF,), 0.5, 3.0, ((0, 32),), jnp.float32)
    down_weight = normal_values(key_of[6], (FF, D), FF ** -0.5, 0.0390625, ((0, 32), (1, 32)))
    down_bias = normal_values(key_of[7], (D,), 0.5, 3.0, ((0, 32),), jnp.float32)
    return {"patches": patches, "frame_counts": frame_counts, "patch_mask": patch_mask, "norm_gain": norm_gain, "up_weight": up_weight, "up_bias": up_bias, "down_weight": down_weight, "down_bias": down_bias}


epsilon = 1e-06

def reference(patches, frame_counts, patch_mask, norm_gain, up_weight, up_bias, down_weight, down_bias):
    values = patches.astype(jnp.float32)
    row_mean = lax.optimization_barrier(jnp.sum(values, axis=1)) / D
    spread = lax.optimization_barrier(jnp.sum(values * values, axis=1)) / D - row_mean * row_mean
    scaled = (values - row_mean[:, None]) * lax.rsqrt(spread + epsilon)[:, None]
    normed = (scaled * norm_gain[None, :]).astype(jnp.bfloat16)
    preact = jnp.dot(normed, up_weight, preferred_element_type=jnp.float32) + up_bias[None, :]
    hidden = jax.nn.gelu(preact, approximate=True).astype(jnp.bfloat16)
    summed = jnp.dot(hidden, down_weight, preferred_element_type=jnp.float32) + down_bias[None, :]
    positions = jnp.arange(TOKENS, dtype=jnp.int32)
    limits = jnp.repeat(frame_counts.astype(jnp.int32), TOK_DEV, total_repeat_length=TOKENS)
    valid_rows = ((positions % TOK_DEV // FRAME_TOK < limits) & (patch_mask == 1)).astype(jnp.float32)
    return (valid_rows[:, None] * summed).astype(jnp.bfloat16)
```

```python
import functools
import math

import jax
import jax.numpy as jnp
from jax import lax
from jax.experimental import pallas as pl
from jax.experimental.pallas import tpu as pltpu
from jax.sharding import PartitionSpec as P

MESH = pl.DeviceIdType.MESH
BF16, F32 = jnp.bfloat16, jnp.float32
FRAME_TOK = 4
EPSILON = 1e-06
NZ, NX, NY = 16, 2, 8
CLIPS = NZ * NX
CHIPS = NY * 2
CHUNKS = 4
ROWS = 12
D_DEV = 192
FF_DEV = 768
HALF = FF_DEV // 2
OWN = 2 * ROWS
D_MODEL = 6144


def tok_peer(tok, k):
    z, column, i = tok % NZ, tok // NZ, k // 2
    step = NZ // 2 + ((i + 1) // 2) * (1 - 2 * (i % 2))
    return ((column + 1 + k % 2) % NX) * NZ + (z + step) % NZ


def chip_peer(chip, k):
    y, column, i = chip // 2, chip % 2, k // 2
    step = NY // 2 + ((i + 1) // 2) * (1 - 2 * (i % 2))
    return ((y + step) % NY) * 2 + (column + 1 + k % 2) % 2


def send(src, dst, send_sem, recv_sem, device):
    pltpu.make_async_remote_copy(
        src_ref=src, dst_ref=dst, send_sem=send_sem, recv_sem=recv_sem, device_id=device, device_id_type=MESH
    ).start()


def settle(ref, sem):
    pltpu.make_async_copy(ref, ref, sem).wait()


def gelu(v):
    return 0.5 * v * (1.0 + jnp.tanh(math.sqrt(2.0 / math.pi) * (v + 0.044715 * (v * v * v))))


def kernel(
    x_hbm, counts, mask, gain, w1_hbm, b1, w2_hbm, b2, out,
    xg, w1c, w2v, gains, gsend, grecv, stsend, strecv, turned, pbuf, precv, hid, qbuf, qrecv,
    local, ws, wr, gs, gr, xs, xr, xfs, xfr, ps, pr, hs, hr, hfs, hfr, qs, qr,
):
    tok, feat = lax.axis_index("tok"), lax.axis_index("feat")
    core, chip = feat % 2, feat // 2
    other = 1 - core
    partner = {"feat": feat + 1 - 2 * core}

    copies = [
        pltpu.make_async_copy(x_hbm, xg.at[core, tok], local.at[0]),
        pltpu.make_async_copy(w1_hbm.at[:, pl.ds(pl.multiple_of(core * HALF, 128), HALF)], w1c.at[core], local.at[1]),
        pltpu.make_async_copy(w2_hbm, w2v, local.at[2]),
    ]
    for copy in copies:
        copy.start()
    gains[pl.ds(core, 1)] = gain[...].reshape(1, 1, D_DEV)

    barrier = pltpu.get_barrier_semaphore()

    @pl.loop(0, CLIPS - 1)
    def _(k):
        pl.semaphore_signal(barrier, inc=1, device_id={"tok": tok_peer(tok, k)}, device_id_type=MESH)

    @pl.loop(0, CHIPS - 1)
    def _(k):
        pl.semaphore_signal(barrier, inc=1, device_id={"feat": chip_peer(chip, k) * 2 + core}, device_id_type=MESH)

    pl.semaphore_signal(barrier, inc=1, device_id=partner, device_id_type=MESH)
    copies[0].wait()
    pl.semaphore_wait(barrier, CLIPS - 1 + CHIPS - 1 + 1)

    send(xg.at[core, tok], xg.at[core, tok], xfs, xfr, partner)

    @pl.loop(0, CLIPS - 1)
    def _(k):
        send(xg.at[core, tok], xg.at[core, tok], xs, xr.at[tok], {"tok": tok_peer(tok, k)})

    send(w1_hbm.at[:, pl.ds(pl.multiple_of(other * HALF, 128), HALF)], w1c.at[core], ws, wr.at[0], partner)
    send(gains.at[core], gains.at[core], gs, wr.at[1], partner)

    copies[1].wait()
    settle(w1c.at[0], wr.at[0])
    settle(gains.at[0], wr.at[1])
    total = jnp.zeros((1, HALF), F32)
    for h in range(2):
        part = gains[h]
        for _ in range(3):
            top = part.astype(BF16)
            total += jnp.dot(jnp.broadcast_to(top, (16, D_DEV)), w1c[h], preferred_element_type=F32)[0:1]
            part = part - top.astype(F32)
    gsend[...] = total

    @pl.loop(0, CHIPS - 1)
    def _(k):
        send(gsend, grecv.at[chip], gs, gr, {"feat": chip_peer(chip, k) * 2 + core})

    own_g = pltpu.make_async_copy(gsend, grecv.at[chip], gr)
    own_g.start()

    @pl.loop(0, CLIPS - 1)
    def _(k):
        source = tok_peer(tok, CLIPS - 2 - k)
        settle(xg.at[core, source], xr.at[source])
        send(xg.at[core, source], xg.at[core, source], xfs, xfr, partner)

    settle(xg.at[0], xfr)

    lane = lax.broadcasted_iota(jnp.int32, (4 * OWN, 128), 1)

    @pl.loop(0, CHUNKS)
    def _(q):
        halves = [[xg[h, q * 8 + i].astype(F32) for i in range(8)] for h in range(2)]
        rows = [jnp.concatenate([jnp.concatenate([v[2 * i], v[2 * i + 1]], axis=0) for i in range(4)], axis=0) for v in halves]
        mean = sum(jnp.sum(r, axis=1, keepdims=True) for r in rows) * (1.0 / (2 * D_DEV))
        square = sum(jnp.sum(r * r, axis=1, keepdims=True) for r in rows)
        product = sum(
            jnp.dot(((rows[h] - mean) * gains[h]).astype(BF16), w1c[h], preferred_element_type=F32) for h in range(2)
        )
        stat = jnp.where(lane == 0, mean, jnp.where(lane == 1, square, 0.0))
        stat = jnp.concatenate([stat, jnp.zeros((128 - 4 * OWN, 128), F32)], axis=0)
        stsend[q] = jnp.transpose(stat)[0:2]
        for i in range(4):
            pbuf[q * 4 + i] = product[OWN * i : OWN * (i + 1)].astype(BF16)
        for i in range(4):
            owner = q * 4 + i

            @pl.when(owner != chip)
            def _():
                send(pbuf.at[owner], precv.at[chip], ps, pr.at[0], {"feat": owner * 2 + core})
                send(stsend.at[q], strecv.at[chip], ps, pr.at[1], {"feat": owner * 2 + core})

            @pl.when(owner == chip)
            def _():
                pltpu.make_async_copy(pbuf.at[owner], precv.at[chip], pr.at[0]).start()
                pltpu.make_async_copy(stsend.at[q], strecv.at[chip], pr.at[1]).start()

    settle(grecv, gr)
    settle(strecv, pr.at[1])
    turned[0] = jnp.transpose(jnp.concatenate([strecv[:, 0, :], jnp.zeros((112, 128), F32)], axis=0))
    turned[1] = jnp.transpose(jnp.concatenate([strecv[:, 1, :], jnp.zeros((112, 128), F32)], axis=0))
    mine = pl.ds(pl.multiple_of((chip % 4) * OWN, 8), OWN)
    means = turned[0, mine]
    mean = jnp.sum(means, axis=1, keepdims=True) * (1.0 / CHIPS)
    spread = jnp.sum(turned[1, mine], axis=1, keepdims=True) * (1.0 / D_MODEL) - mean * mean
    settle(precv, pr.at[0])
    acc = jnp.zeros((OWN, HALF), F32)
    for s in range(CHIPS):
        acc += precv[s].astype(F32) + (means[:, s : s + 1] - mean) * grecv[s]
    bias = b1[pl.ds(pl.multiple_of(core * HALF, 128), HALF)].reshape(1, HALF)
    hid[core, chip] = gelu(acc * lax.rsqrt(spread + EPSILON) + bias).astype(BF16)

    @pl.loop(0, CHIPS - 1)
    def _(k):
        send(hid.at[core, chip], hid.at[core, chip], hs, hr.at[chip], {"feat": chip_peer(chip, k) * 2 + core})

    send(hid.at[core, chip], hid.at[core, chip], hfs, hfr, partner)

    @pl.loop(0, CHIPS - 1)
    def _(k):
        source = chip_peer(chip, CHIPS - 2 - k)
        settle(hid.at[core, source], hr.at[source])
        send(hid.at[core, source], hid.at[core, source], hfs, hfr, partner)

    copies[2].wait()
    settle(hid.at[0], hfr)

    @pl.loop(0, CHUNKS)
    def _(q):
        rows = [jnp.concatenate([hid[h, q * 4 + i].astype(F32) for i in range(4)], axis=0).astype(BF16) for h in range(2)]
        product = sum(jnp.dot(rows[h], w2v[h * HALF : (h + 1) * HALF], preferred_element_type=F32) for h in range(2))
        for i in range(8):
            qbuf[q * 8 + i] = product[ROWS * i : ROWS * (i + 1)].astype(BF16)
        for i in range(8):
            clip = q * 8 + i

            @pl.when(clip != tok)
            def _():
                send(qbuf.at[clip], qrecv.at[tok], qs, qr, {"tok": clip})

            @pl.when(clip == tok)
            def _():
                pltpu.make_async_copy(qbuf.at[clip], qrecv.at[tok], qr).start()

    position = lax.broadcasted_iota(jnp.int32, (ROWS, 1), 0)
    kept = jnp.zeros((ROWS, 1), jnp.int32)
    for r in range(ROWS):
        kept = jnp.where(position == r, mask[r], kept)
    valid = jnp.where((position // FRAME_TOK < counts[0]) & (kept == 1), 1.0, 0.0)
    settle(qrecv, qr)
    acc = qrecv[0].astype(F32)
    for s in range(1, CLIPS):
        acc += qrecv[s].astype(F32)
    out[...] = (valid * (acc + b2[...].reshape(1, D_DEV))).astype(BF16)

    settle(w1c.at[0], ws)
    settle(gains.at[0], gs)
    settle(grecv.at[pl.ds(0, CHIPS - 1)], gs)
    settle(xg.at[0, pl.ds(0, CLIPS - 1)], xs)
    settle(xg.at[0], xfs)
    settle(pbuf.at[pl.ds(0, CHIPS - 1)], ps)
    settle(strecv.at[pl.ds(0, CHIPS - 1)], ps)
    settle(hid.at[0, pl.ds(0, CHIPS - 1)], hs)
    settle(hid.at[0], hfs)
    settle(qbuf.at[pl.ds(0, CLIPS - 1)], qs)


def per_device(patches, frame_counts, patch_mask, norm_gain, up_weight, up_bias, down_weight, down_bias):
    vmem, smem, hbm = (pl.BlockSpec(memory_space=m) for m in (pltpu.VMEM, pltpu.SMEM, pl.ANY))
    dma = pltpu.SemaphoreType.DMA
    return pl.pallas_call(
        kernel,
        out_shape=jax.ShapeDtypeStruct(patches.shape, BF16),
        in_specs=[hbm, smem, smem, vmem, hbm, vmem, hbm, vmem],
        out_specs=vmem,
        scratch_shapes=[
            pltpu.VMEM((2, CLIPS, ROWS, D_DEV), BF16),
            pltpu.VMEM((2, D_DEV, HALF), BF16),
            pltpu.VMEM((FF_DEV, D_DEV), BF16),
            pltpu.VMEM((2, 1, D_DEV), F32),
            pltpu.VMEM((1, HALF), F32),
            pltpu.VMEM((CHIPS, 1, HALF), F32),
            pltpu.VMEM((CHUNKS, 2, 128), F32),
            pltpu.VMEM((CHIPS, 2, 128), F32),
            pltpu.VMEM((2, 128, 128), F32),
            pltpu.VMEM((CHIPS, OWN, HALF), BF16),
            pltpu.VMEM((CHIPS, OWN, HALF), BF16),
            pltpu.VMEM((2, CHIPS, OWN, HALF), BF16),
            pltpu.VMEM((CLIPS, ROWS, D_DEV), BF16),
            pltpu.VMEM((CLIPS, ROWS, D_DEV), BF16),
            dma((3,)), dma, dma((2,)), dma, dma, dma, dma((CLIPS,)), dma, dma,
            dma, dma((2,)), dma, dma((CHIPS,)), dma, dma, dma, dma,
        ],
        compiler_params=pltpu.CompilerParams(collective_id=0, has_side_effects=True),
        name="mlp",
    )(patches, frame_counts, patch_mask, norm_gain, up_weight, up_bias, down_weight, down_bias)


def solution(mesh):
    in_specs = (
        P("tok", "feat"), P("tok"), P("tok"), P("feat"), P("feat", "tok"), P("tok"), P("tok", "feat"), P("feat"),
    )
    return jax.shard_map(per_device, mesh=mesh, in_specs=in_specs, out_specs=P("tok", "feat"), check_vma=False)
```

```python
import functools
import math

import jax
import jax.numpy as jnp
from jax import lax
from jax.experimental import pallas as pl
from jax.experimental.pallas import tpu as pltpu
from jax.sharding import PartitionSpec as P

MESH = pl.DeviceIdType.MESH
BF16, F32 = jnp.bfloat16, jnp.float32
FRAME_TOK = 4
EPSILON = 1e-06
NZ, NX, NY = 16, 2, 8
CLIPS = NZ * NX
CHIPS = NY * 2
CHUNKS = 4
ROWS = 12
D_DEV = 192
FF_DEV = 768
HALF = FF_DEV // 2
OWN = 2 * ROWS
D_MODEL = 6144
CLOSE = [(step, flip) for step in (2, -2, 1, -1, 0) for flip in (1, 0) if step or flip]


def mod(a, n):
    return lax.rem(a + n, n)


def chip_peer(chip, k):
    y, column, i = lax.div(chip, 2), lax.rem(chip, 2), lax.div(k, 2)
    step = NY // 2 + lax.div(i + 1, 2) * (1 - 2 * lax.rem(i, 2))
    return mod(y + step, NY) * 2 + lax.rem(column + 1 + lax.rem(k, 2), 2)


def send(src, dst, send_sem, recv_sem, device):
    pltpu.make_async_remote_copy(
        src_ref=src, dst_ref=dst, send_sem=send_sem, recv_sem=recv_sem, device_id=device, device_id_type=MESH
    ).start()


def settle(ref, sem):
    pltpu.make_async_copy(ref, ref, sem).wait()


def gelu(v):
    return 0.5 * v * (1.0 + jnp.tanh(math.sqrt(2.0 / math.pi) * (v + 0.044715 * (v * v * v))))


def kernel(
    x_hbm, counts_hbm, mask_hbm, gain_hbm, w1_hbm, b1_hbm, w2_hbm, b2_hbm, out,
    xv, counts, mask, b1, b2, outv, xg, w1c, w2v, gains, gsend, grecv, stsend, strecv, turned, pbuf, precv, hid, qbuf, qrecv,
    local, ws, wr, gs, gr, xs, xr, xfs, xfr, here, ps, pr, hs, hr, hfs, hfr, qs, qr,
):
    tok, feat = lax.axis_index("tok"), lax.axis_index("feat")
    z, column = lax.rem(tok, NZ), lax.div(tok, NZ)
    core, chip = lax.rem(feat, 2), lax.div(feat, 2)
    x, y = lax.rem(chip, 2) * 2 + column, lax.div(chip, 2)
    other = 1 - core
    partner = {"feat": feat + 1 - 2 * core}

    def local_copy(i, src, dst):
        copy = pltpu.make_async_copy(src, dst, local.at[i])
        copy.start()
        return copy

    x_in = local_copy(0, x_hbm, xv)
    gain_in = local_copy(1, gain_hbm, gains.at[core, 0])
    w1_in = local_copy(2, w1_hbm.at[:, pl.ds(pl.multiple_of(core * HALF, 128), HALF)], w1c.at[core])
    small_in = [local_copy(3 + i, *pair) for i, pair in enumerate(((b1_hbm, b1), (b2_hbm, b2), (counts_hbm, counts), (mask_hbm, mask)))]
    w2_in = local_copy(7, w2_hbm, w2v)

    def clip_at(step, c):
        return c * NZ + mod(z + step, NZ)

    def chip_at(step, flip):
        column2 = lax.rem(chip + flip, 2)
        return mod(y + step, NY) * 2 + column2

    barrier = pltpu.get_barrier_semaphore()

    def greet(device):
        pl.semaphore_signal(barrier, inc=1, device_id=device, device_id_type=MESH)

    steps = [d * sign for d in (4, 3, 2, 1) for sign in (1, -1)]
    for step in steps:
        for c in range(NX):
            greet({"tok": clip_at(step, c)})
    for step, flip in CLOSE:
        greet({"feat": chip_at(step, flip) * 2 + core})
    beside = (1 - column) * NZ + z
    greet({"tok": beside})
    greet(partner)

    x_in.wait()
    rows = xv[...].astype(F32)
    for i in range(3):
        xg[core, tok, i] = rows[4 * i : 4 * i + 4].astype(BF16)
    pl.semaphore_wait(barrier, 2 * len(steps) + len(CLOSE) + 2)

    def push(source, target):
        send(xg.at[core, source], xg.at[core, source], xs, xr.at[source], {"tok": target})

    def pass_on(source):
        send(xg.at[core, source], xg.at[core, source], xfs, xfr, partner)

    def arrive(source):
        settle(xg.at[core, source], xr.at[source])

    for step in steps:
        for c in range(NX):
            push(tok, clip_at(step, c))
    push(tok, beside)
    pass_on(tok)
    send(w1_hbm.at[:, pl.ds(pl.multiple_of(other * HALF, 128), HALF)], w1c.at[core], ws, wr.at[0], partner)
    gain_in.wait()
    send(gains.at[core], gains.at[core], gs, wr.at[1], partner)
    for i, step in enumerate((-2, 2)):
        pl.semaphore_signal(here.at[1 - i], inc=1, device_id={"feat": chip_at(step, 0) * 2 + core}, device_id_type=MESH)

    for source in [beside] + [clip_at(sign * d, c) for d in (1, 2, 3) for sign in (1, -1) for c in range(NX)]:
        arrive(source)
        pass_on(source)
    for c in range(NX):
        arrive(clip_at(-4, c))
        for step in (4, 3, 2, 1):
            push(clip_at(-4, c), clip_at(step, column))
    for c in range(NX):
        arrive(clip_at(4, c))
        for step in (-3, -2, -1):
            push(clip_at(4, c), clip_at(step, column))
    for c in range(NX):
        pass_on(clip_at(-4, c))
        pass_on(clip_at(4, c))

    for i in range(2):
        pl.semaphore_wait(here.at[i], 1)

    w1_in.wait()
    settle(w1c.at[0], wr.at[0])
    settle(gains.at[0], wr.at[1])
    total = jnp.zeros((1, HALF), F32)
    for h in range(2):
        part = gains[h]
        for _ in range(3):
            top = part.astype(BF16)
            total += jnp.dot(jnp.broadcast_to(top, (16, D_DEV)), w1c[h], preferred_element_type=F32)[0:1]
            part = part - top.astype(F32)
    gsend[...] = total

    @pl.loop(0, CHIPS - 1)
    def _(k):
        send(gsend, grecv.at[chip], gs, gr, {"feat": chip_peer(chip, k) * 2 + core})

    own_g = pltpu.make_async_copy(gsend, grecv.at[chip], gr)
    own_g.start()

    for source in [clip_at(sign * d, c) for d in (5, 6, 7) for sign in (1, -1) for c in range(NX)] + [clip_at(8, c) for c in range(NX)]:
        arrive(source)
        pass_on(source)
    settle(xg.at[0], xfr)

    lane = lax.broadcasted_iota(jnp.int32, (4 * OWN, 128), 1)

    @pl.loop(0, CHUNKS)
    def _(q):
        rows = [
            jnp.concatenate([xg[h, q * 8 + i, j].astype(F32) for i in range(8) for j in range(3)], axis=0) for h in range(2)
        ]
        mean = sum(jnp.sum(r, axis=1, keepdims=True) for r in rows) * (1.0 / (2 * D_DEV))
        square = sum(jnp.sum(r * r, axis=1, keepdims=True) for r in rows)
        product = sum(
            jnp.dot(((rows[h] - mean) * gains[h]).astype(BF16), w1c[h], preferred_element_type=F32) for h in range(2)
        )
        stat = jnp.where(lane == 0, mean, jnp.where(lane == 1, square, 0.0))
        stat = jnp.concatenate([stat, jnp.zeros((128 - 4 * OWN, 128), F32)], axis=0)
        stsend[q] = jnp.transpose(stat)[0:2]
        for i in range(4):
            pbuf[q * 4 + i] = product[OWN * i : OWN * (i + 1)].astype(BF16)
        for i in range(4):
            owner = q * 4 + i

            @pl.when(owner != chip)
            def _():
                send(pbuf.at[owner], precv.at[chip], ps, pr.at[0], {"feat": owner * 2 + core})
                send(stsend.at[q], strecv.at[chip], ps, pr.at[1], {"feat": owner * 2 + core})

            @pl.when(owner == chip)
            def _():
                pltpu.make_async_copy(pbuf.at[owner], precv.at[chip], pr.at[0]).start()
                pltpu.make_async_copy(stsend.at[q], strecv.at[chip], pr.at[1]).start()

    settle(xg.at[0, pl.ds(0, CLIPS - 1)], xs)

    settle(grecv, gr)
    settle(strecv, pr.at[1])
    turned[0] = jnp.transpose(jnp.concatenate([strecv[:, 0, :], jnp.zeros((112, 128), F32)], axis=0))
    turned[1] = jnp.transpose(jnp.concatenate([strecv[:, 1, :], jnp.zeros((112, 128), F32)], axis=0))
    mine = pl.ds(pl.multiple_of((chip % 4) * OWN, 8), OWN)
    means = turned[0, mine]
    mean = jnp.sum(means, axis=1, keepdims=True) * (1.0 / CHIPS)
    spread = jnp.sum(turned[1, mine], axis=1, keepdims=True) * (1.0 / D_MODEL) - mean * mean
    settle(precv, pr.at[0])
    acc = jnp.zeros((OWN, HALF), F32)
    for s in range(CHIPS):
        acc += precv[s].astype(F32) + (means[:, s : s + 1] - mean) * grecv[s]
    small_in[0].wait()
    bias = b1[pl.ds(pl.multiple_of(core * HALF, 128), HALF)].reshape(1, HALF)
    hid[core, chip] = gelu(acc * lax.rsqrt(spread + EPSILON) + bias).astype(BF16)

    @pl.loop(0, CHIPS - 1)
    def _(k):
        send(hid.at[core, chip], hid.at[core, chip], hs, hr.at[chip], {"feat": chip_peer(chip, k) * 2 + core})

    send(hid.at[core, chip], hid.at[core, chip], hfs, hfr, partner)

    @pl.loop(0, CHIPS - 1)
    def _(k):
        source = chip_peer(chip, CHIPS - 2 - k)
        settle(hid.at[core, source], hr.at[source])
        send(hid.at[core, source], hid.at[core, source], hfs, hfr, partner)

    w2_in.wait()
    settle(hid.at[0], hfr)

    @pl.loop(0, CHUNKS)
    def _(q):
        rows = [jnp.concatenate([hid[h, q * 4 + i].astype(F32) for i in range(4)], axis=0).astype(BF16) for h in range(2)]
        product = sum(
            lax.dot_general(
                rows[h], w2v[:, h * HALF : (h + 1) * HALF], (((1,), (1,)), ((), ())), preferred_element_type=F32
            )
            for h in range(2)
        )
        ahead = pltpu.roll(product[:, 128:], 4 * OWN - 6, 0)
        narrow = jnp.concatenate([product[:, 128:], ahead], axis=1)
        for i in range(8):
            packed = [product[ROWS * i : ROWS * (i + 1), :128], narrow[ROWS * i : ROWS * i + 6], jnp.zeros((6, 128), F32)]
            qbuf[q * 8 + i] = jnp.concatenate(packed, axis=0).astype(BF16)
        for i in range(8):
            clip = q * 8 + i

            @pl.when(clip != tok)
            def _():
                send(qbuf.at[clip], qrecv.at[tok], qs, qr, {"tok": clip})

            @pl.when(clip == tok)
            def _():
                pltpu.make_async_copy(qbuf.at[clip], qrecv.at[tok], qr).start()

    for copy in small_in[1:]:
        copy.wait()
    position = lax.broadcasted_iota(jnp.int32, (ROWS, ROWS), 0)
    lane = lax.broadcasted_iota(jnp.int32, (ROWS, ROWS), 1)
    kept = jnp.where(position == lane, jnp.broadcast_to(mask[...].reshape(1, ROWS), (ROWS, ROWS)), 0)
    kept = jnp.sum(kept.astype(F32), axis=1, keepdims=True)
    present = jnp.broadcast_to(counts[...].reshape(1, 1), (ROWS, 1)) > lax.div(position[:, :1], FRAME_TOK)
    valid = jnp.where(present & (kept == 1.0), 1.0, 0.0)
    settle(qrecv, qr)
    acc = qrecv[0].astype(F32)
    for s in range(1, CLIPS):
        acc += qrecv[s].astype(F32)
    narrow = jnp.concatenate([acc[12:18, :64], acc[12:18, 64:]], axis=0)
    acc = jnp.concatenate([acc[:ROWS], narrow], axis=1)
    outv[...] = (valid * (acc + b2[...].reshape(1, D_DEV))).astype(BF16)

    result = local_copy(8, outv, out)

    settle(w1c.at[0], ws)
    settle(gains.at[0], gs)
    settle(grecv.at[pl.ds(0, CHIPS - 1)], gs)
    settle(xg.at[0], xfs)
    settle(pbuf.at[pl.ds(0, CHIPS - 1)], ps)
    settle(strecv.at[pl.ds(0, CHIPS - 1)], ps)
    settle(hid.at[0, pl.ds(0, CHIPS - 1)], hs)
    settle(hid.at[0], hfs)
    settle(qbuf.at[pl.ds(0, CLIPS - 1)], qs)
    result.wait()


def per_device(patches, frame_counts, patch_mask, norm_gain, up_weight, up_bias, down_weight, down_bias):
    hbm = pl.BlockSpec(memory_space=pltpu.HBM)
    dma = pltpu.SemaphoreType.DMA
    return pl.pallas_call(
        kernel,
        out_shape=jax.ShapeDtypeStruct(patches.shape, BF16),
        in_specs=[hbm] * 8,
        out_specs=hbm,
        scratch_shapes=[
            pltpu.VMEM((ROWS, D_DEV), BF16),
            pltpu.VMEM((1,), jnp.int32),
            pltpu.VMEM((ROWS,), jnp.int32),
            pltpu.VMEM((FF_DEV,), F32),
            pltpu.VMEM((D_DEV,), F32),
            pltpu.VMEM((ROWS, D_DEV), BF16),
            pltpu.VMEM((2, CLIPS, 3, 4, D_DEV), BF16),
            pltpu.VMEM((2, D_DEV, HALF), BF16),
            pltpu.VMEM((D_DEV, FF_DEV), BF16),
            pltpu.VMEM((2, 1, D_DEV), F32),
            pltpu.VMEM((1, HALF), F32),
            pltpu.VMEM((CHIPS, 1, HALF), F32),
            pltpu.VMEM((CHUNKS, 2, 128), F32),
            pltpu.VMEM((CHIPS, 2, 128), F32),
            pltpu.VMEM((2, 128, 128), F32),
            pltpu.VMEM((CHIPS, OWN, HALF), BF16),
            pltpu.VMEM((CHIPS, OWN, HALF), BF16),
            pltpu.VMEM((2, CHIPS, OWN, HALF), BF16),
            pltpu.VMEM((CLIPS, 24, 128), BF16),
            pltpu.VMEM((CLIPS, 24, 128), BF16),
            dma((9,)), dma, dma((2,)), dma, dma, dma, dma((CLIPS,)), dma, dma, pltpu.SemaphoreType.REGULAR((2,)),
            dma, dma((2,)), dma, dma((CHIPS,)), dma, dma, dma, dma,
        ],
        compiler_params=pltpu.CompilerParams(collective_id=0, has_side_effects=True),
        name="mlp",
    )(patches, frame_counts, patch_mask, norm_gain, up_weight, up_bias, down_weight.T, down_bias)


def solution(mesh):
    in_specs = (
        P("tok", "feat"), P("tok"), P("tok"), P("feat"), P("feat", "tok"), P("tok"), P("tok", "feat"), P("feat"),
    )
    return jax.shard_map(per_device, mesh=mesh, in_specs=in_specs, out_specs=P("tok", "feat"), check_vma=False)
```

```python
import functools
import math

import jax
import jax.numpy as jnp
from jax import lax
from jax.experimental import pallas as pl
from jax.experimental.pallas import tpu as pltpu
from jax.sharding import PartitionSpec as P

MESH = pl.DeviceIdType.MESH
BF16, F32 = jnp.bfloat16, jnp.float32
FRAME_TOK = 4
EPSILON = 1e-06
NZ, NX, NY = 16, 2, 8
CLIPS = NZ * NX
CHIPS = NY * 2
CHUNKS = 4
ROWS = 12
D_DEV = 192
FF_DEV = 768
HALF = FF_DEV // 2
OWN = 2 * ROWS
D_MODEL = 6144
CLOSE = [(step, flip) for step in (2, -2, 1, -1, 0) for flip in (1, 0) if step or flip]


def mod(a, n):
    return lax.rem(a + n, n)


def chip_peer(chip, k):
    y, column, i = lax.div(chip, 2), lax.rem(chip, 2), lax.div(k, 2)
    step = NY // 2 + lax.div(i + 1, 2) * (1 - 2 * lax.rem(i, 2))
    return mod(y + step, NY) * 2 + lax.rem(column + 1 + lax.rem(k, 2), 2)


def send(src, dst, send_sem, recv_sem, device):
    pltpu.make_async_remote_copy(
        src_ref=src, dst_ref=dst, send_sem=send_sem, recv_sem=recv_sem, device_id=device, device_id_type=MESH
    ).start()


def settle(ref, sem):
    pltpu.make_async_copy(ref, ref, sem).wait()


def gelu(v):
    return 0.5 * v * (1.0 + jnp.tanh(math.sqrt(2.0 / math.pi) * (v + 0.044715 * (v * v * v))))


def kernel(
    x_hbm, counts_hbm, mask_hbm, gain_hbm, w1_hbm, b1_hbm, w2_hbm, b2_hbm, out,
    xv, counts, mask, b1, b2, outv, xg, w1c, w2v, gains, gsend, grecv, stsend, strecv, turned, pbuf, precv, hid, qbuf, qrecv, qtail, qrtail,
    local, ws, wr, gs, gr, xs, xr, xfs, xfr, here, ps, pr, hs, hr, hfs, hfr, qs, qr,
):
    tok, feat = lax.axis_index("tok"), lax.axis_index("feat")
    z, column = lax.rem(tok, NZ), lax.div(tok, NZ)
    core, chip = lax.rem(feat, 2), lax.div(feat, 2)
    x, y = lax.rem(chip, 2) * 2 + column, lax.div(chip, 2)
    other = 1 - core
    partner = {"feat": feat + 1 - 2 * core}

    def local_copy(i, src, dst):
        copy = pltpu.make_async_copy(src, dst, local.at[i])
        copy.start()
        return copy

    x_in = local_copy(0, x_hbm, xv)
    gain_in = local_copy(1, gain_hbm, gains.at[core, 0])
    w1_in = local_copy(2, w1_hbm.at[:, pl.ds(pl.multiple_of(core * HALF, 128), HALF)], w1c.at[core])
    small_in = [local_copy(3 + i, *pair) for i, pair in enumerate(((b1_hbm, b1), (b2_hbm, b2), (counts_hbm, counts), (mask_hbm, mask)))]
    w2_in = local_copy(7, w2_hbm, w2v)

    def clip_at(step, c):
        return c * NZ + mod(z + step, NZ)

    def chip_at(step, flip):
        column2 = lax.rem(chip + flip, 2)
        return mod(y + step, NY) * 2 + column2

    barrier = pltpu.get_barrier_semaphore()

    def greet(device):
        pl.semaphore_signal(barrier, inc=1, device_id=device, device_id_type=MESH)

    steps = [d * sign for d in (4, 3, 2, 1) for sign in (1, -1)]
    for step in steps:
        for c in range(NX):
            greet({"tok": clip_at(step, c)})
    for step, flip in CLOSE:
        greet({"feat": chip_at(step, flip) * 2 + core})
    beside = (1 - column) * NZ + z
    greet({"tok": beside})
    greet(partner)

    x_in.wait()
    rows = xv[...].astype(F32)
    for i in range(3):
        xg[core, tok, i] = rows[4 * i : 4 * i + 4].astype(BF16)
    pl.semaphore_wait(barrier, 2 * len(steps) + len(CLOSE) + 2)

    def push(source, target):
        send(xg.at[core, source], xg.at[core, source], xs, xr.at[source], {"tok": target})

    def pass_on(source, far):
        send(xg.at[core, source], xg.at[core, source], xfs, xfr.at[far], partner)

    def arrive(source):
        settle(xg.at[core, source], xr.at[source])

    for step in steps:
        for c in range(NX):
            push(tok, clip_at(step, c))
    push(tok, beside)
    pass_on(tok, 0)
    send(w1_hbm.at[:, pl.ds(pl.multiple_of(other * HALF, 128), HALF)], w1c.at[core], ws, wr.at[0], partner)
    gain_in.wait()
    send(gains.at[core], gains.at[core], gs, wr.at[1], partner)
    for i, step in enumerate((-2, 2)):
        pl.semaphore_signal(here.at[1 - i], inc=1, device_id={"feat": chip_at(step, 0) * 2 + core}, device_id_type=MESH)

    for source in [beside] + [clip_at(sign * d, c) for d in (1, 2, 3) for sign in (1, -1) for c in range(NX)]:
        arrive(source)
        pass_on(source, 0)
    for c in range(NX):
        arrive(clip_at(-4, c))
        for step in (4, 3, 2, 1):
            push(clip_at(-4, c), clip_at(step, column))
    for c in range(NX):
        arrive(clip_at(4, c))
        for step in (-3, -2, -1):
            push(clip_at(4, c), clip_at(step, column))
    for c in range(NX):
        pass_on(clip_at(-4, c), lax.rem(z, 2))
        pass_on(clip_at(4, c), 1 - lax.rem(z, 2))

    for i in range(2):
        pl.semaphore_wait(here.at[i], 1)

    w1_in.wait()
    settle(w1c.at[0], wr.at[0])
    settle(gains.at[0], wr.at[1])
    total = jnp.zeros((1, HALF), F32)
    for h in range(2):
        part = gains[h]
        for _ in range(3):
            top = part.astype(BF16)
            total += jnp.dot(jnp.broadcast_to(top, (16, D_DEV)), w1c[h], preferred_element_type=F32)[0:1]
            part = part - top.astype(F32)
    gsend[...] = total

    @pl.loop(0, CHIPS - 1)
    def _(k):
        send(gsend, grecv.at[chip], gs, gr, {"feat": chip_peer(chip, k) * 2 + core})

    own_g = pltpu.make_async_copy(gsend, grecv.at[chip], gr)
    own_g.start()

    lane = lax.broadcasted_iota(jnp.int32, (4 * OWN, 128), 1)
    base = 2 * lax.div(z + 1, 2) - 4

    def first_product(far):
        settle(xg.at[0, pl.ds(0, CLIPS // 2)], xfr.at[far])

        @pl.loop(0, NX)
        def _(c):
            q = far * NX + c
            clips = [c * NZ + mod(base + 8 * far + i, NZ) for i in range(8)]
            rows = [
                jnp.concatenate([xg[h, clip, j].astype(F32) for clip in clips for j in range(3)], axis=0) for h in range(2)
            ]
            mean = sum(jnp.sum(r, axis=1, keepdims=True) for r in rows) * (1.0 / (2 * D_DEV))
            square = sum(jnp.sum(r * r, axis=1, keepdims=True) for r in rows)
            product = sum(
                jnp.dot(((rows[h] - mean) * gains[h]).astype(BF16), w1c[h], preferred_element_type=F32) for h in range(2)
            )
            owners = [c * (CHIPS // 2) + mod(lax.div(base, 2) + 4 * far + i, CHIPS // 2) for i in range(4)]
            for i, owner in enumerate(owners):
                pbuf[owner] = product[OWN * i : OWN * (i + 1)].astype(BF16)
            stat = jnp.where(lane == 0, mean, jnp.where(lane == 1, square, 0.0))
            stat = jnp.concatenate([stat, jnp.zeros((128 - 4 * OWN, 128), F32)], axis=0)
            stsend[q] = jnp.transpose(stat)[0:2]
            for owner in owners:

                @pl.when(owner != chip)
                def _():
                    send(pbuf.at[owner], precv.at[chip], ps, pr.at[0], {"feat": owner * 2 + core})
                    send(stsend.at[q], strecv.at[chip], ps, pr.at[1], {"feat": owner * 2 + core})

                @pl.when(owner == chip)
                def _():
                    pltpu.make_async_copy(pbuf.at[owner], precv.at[chip], pr.at[0]).start()
                    pltpu.make_async_copy(stsend.at[q], strecv.at[chip], pr.at[1]).start()

    first_product(0)
    for source in [clip_at(sign * d, c) for d in (5, 6, 7) for sign in (1, -1) for c in range(NX)] + [clip_at(8, c) for c in range(NX)]:
        arrive(source)
        pass_on(source, 1)

    first_product(1)
    settle(xg.at[0, pl.ds(0, CLIPS - 1)], xs)

    settle(grecv, gr)
    settle(strecv, pr.at[1])
    turned[0] = jnp.transpose(jnp.concatenate([strecv[:, 0, :], jnp.zeros((112, 128), F32)], axis=0))
    turned[1] = jnp.transpose(jnp.concatenate([strecv[:, 1, :], jnp.zeros((112, 128), F32)], axis=0))
    place = lax.rem(lax.rem(chip, CHIPS // 2) - lax.div(base, 2) + CHIPS, 4)
    mine = pl.ds(pl.multiple_of(place * OWN, 8), OWN)
    means = turned[0, mine]
    mean = jnp.sum(means, axis=1, keepdims=True) * (1.0 / CHIPS)
    spread = jnp.sum(turned[1, mine], axis=1, keepdims=True) * (1.0 / D_MODEL) - mean * mean
    settle(precv, pr.at[0])
    acc = jnp.zeros((OWN, HALF), F32)
    for s in range(CHIPS):
        acc += precv[s].astype(F32) + (means[:, s : s + 1] - mean) * grecv[s]
    small_in[0].wait()
    bias = b1[pl.ds(pl.multiple_of(core * HALF, 128), HALF)].reshape(1, HALF)
    hid[core, chip] = gelu(acc * lax.rsqrt(spread + EPSILON) + bias).astype(BF16)

    def block_to(source, device_chip):
        send(hid.at[core, source], hid.at[core, source], hs, hr.at[source], {"feat": device_chip * 2 + core})

    for step, flip in CLOSE:
        block_to(chip, chip_at(step, flip))
    send(hid.at[core, chip], hid.at[core, chip], hfs, hfr.at[0], partner)

    places = (
        ((0, 0), (1, 0), (-1, 0), (0, 1)),
        ((2, 0), (-2, 0), (1, 1), (-1, 1)),
        ((2, 1), (-2, 1), (3, 0), (-3, 0)),
        ((4, 0), (3, 1), (-3, 1), (4, 1)),
    )
    groups = [[chip_at(*place) for place in group] for group in places]

    def collect(g, first, last):
        for place in places[g][first:last]:
            source = chip_at(*place)
            settle(hid.at[core, source], hr.at[source])
            for step in {-2: (1, 2), 2: (-1,)}.get(place[0], ()):
                block_to(source, chip_at(step, 0))
            send(hid.at[core, source], hid.at[core, source], hfs, hfr.at[g], partner)

    def second_product(g):
        settle(hid.at[0, pl.ds(0, 4)], hfr.at[g])
        rows = [jnp.concatenate([hid[h, owner].astype(F32) for owner in groups[g]], axis=0).astype(BF16) for h in range(2)]
        product = sum(
            lax.dot_general(
                rows[h], w2v[:, h * HALF : (h + 1) * HALF], (((1,), (1,)), ((), ())), preferred_element_type=F32
            )
            for h in range(2)
        )
        ahead = pltpu.roll(product[:, 128:], 4 * OWN - 6, 0)
        narrow = jnp.concatenate([product[:, 128:], ahead], axis=1)
        clips = [2 * owner + e for owner in groups[g] for e in range(2)]
        for i, clip in enumerate(clips):
            packed = [product[ROWS * i : ROWS * (i + 1), :128], narrow[ROWS * i : ROWS * i + 4]]
            qbuf[clip] = jnp.concatenate(packed, axis=0).astype(BF16)
            qtail[clip] = narrow[ROWS * i + 4 : ROWS * i + 6].astype(BF16)
        for clip in clips:

            @pl.when(clip != tok)
            def _():
                send(qbuf.at[clip], qrecv.at[tok], qs, qr.at[0], {"tok": clip})
                send(qtail.at[clip], qrtail.at[tok], qs, qr.at[1], {"tok": clip})

            @pl.when(clip == tok)
            def _():
                pltpu.make_async_copy(qbuf.at[clip], qrecv.at[tok], qr.at[0]).start()
                pltpu.make_async_copy(qtail.at[clip], qrtail.at[tok], qr.at[1]).start()

    w2_in.wait()
    collect(0, 1, 4)
    collect(1, 0, 4)
    collect(2, 0, 2)
    second_product(0)
    second_product(1)
    collect(2, 2, 4)
    second_product(2)
    collect(3, 0, 4)
    second_product(3)

    for copy in small_in[1:]:
        copy.wait()
    position = lax.broadcasted_iota(jnp.int32, (ROWS, ROWS), 0)
    lane = lax.broadcasted_iota(jnp.int32, (ROWS, ROWS), 1)
    kept = jnp.where(position == lane, jnp.broadcast_to(mask[...].reshape(1, ROWS), (ROWS, ROWS)), 0)
    kept = jnp.sum(kept.astype(F32), axis=1, keepdims=True)
    present = jnp.broadcast_to(counts[...].reshape(1, 1), (ROWS, 1)) > lax.div(position[:, :1], FRAME_TOK)
    valid = jnp.where(present & (kept == 1.0), 1.0, 0.0)
    settle(qrtail, qr.at[1])
    settle(qrecv, qr.at[0])
    acc, tail = qrecv[0].astype(F32), qrtail[0].astype(F32)
    for s in range(1, CLIPS):
        acc += qrecv[s].astype(F32)
        tail += qrtail[s].astype(F32)
    acc = jnp.concatenate([acc, tail], axis=0)
    narrow = jnp.concatenate([acc[12:18, :64], acc[12:18, 64:]], axis=0)
    acc = jnp.concatenate([acc[:ROWS], narrow], axis=1)
    outv[...] = (valid * (acc + b2[...].reshape(1, D_DEV))).astype(BF16)

    result = local_copy(8, outv, out)

    settle(w1c.at[0], ws)
    settle(gains.at[0], gs)
    settle(grecv.at[pl.ds(0, CHIPS - 1)], gs)
    settle(xg.at[0], xfs)
    settle(pbuf.at[pl.ds(0, CHIPS - 1)], ps)
    settle(strecv.at[pl.ds(0, CHIPS - 1)], ps)
    settle(hid.at[0, pl.ds(0, CHIPS - 1)], hs)
    settle(hid.at[0], hfs)
    settle(qbuf.at[pl.ds(0, CLIPS - 1)], qs)
    settle(qtail.at[pl.ds(0, CLIPS - 1)], qs)
    result.wait()


def per_device(patches, frame_counts, patch_mask, norm_gain, up_weight, up_bias, down_weight, down_bias):
    hbm = pl.BlockSpec(memory_space=pltpu.HBM)
    dma = pltpu.SemaphoreType.DMA
    return pl.pallas_call(
        kernel,
        out_shape=jax.ShapeDtypeStruct(patches.shape, BF16),
        in_specs=[hbm] * 8,
        out_specs=hbm,
        scratch_shapes=[
            pltpu.VMEM((ROWS, D_DEV), BF16),
            pltpu.VMEM((1,), jnp.int32),
            pltpu.VMEM((ROWS,), jnp.int32),
            pltpu.VMEM((FF_DEV,), F32),
            pltpu.VMEM((D_DEV,), F32),
            pltpu.VMEM((ROWS, D_DEV), BF16),
            pltpu.VMEM((2, CLIPS, 3, 4, D_DEV), BF16),
            pltpu.VMEM((2, D_DEV, HALF), BF16),
            pltpu.VMEM((D_DEV, FF_DEV), BF16),
            pltpu.VMEM((2, 1, D_DEV), F32),
            pltpu.VMEM((1, HALF), F32),
            pltpu.VMEM((CHIPS, 1, HALF), F32),
            pltpu.VMEM((CHUNKS, 2, 128), F32),
            pltpu.VMEM((CHIPS, 2, 128), F32),
            pltpu.VMEM((2, 128, 128), F32),
            pltpu.VMEM((CHIPS, OWN, HALF), BF16),
            pltpu.VMEM((CHIPS, OWN, HALF), BF16),
            pltpu.VMEM((2, CHIPS, OWN, HALF), BF16),
            pltpu.VMEM((CLIPS, 16, 128), BF16),
            pltpu.VMEM((CLIPS, 16, 128), BF16),
            pltpu.VMEM((CLIPS, 2, 128), BF16),
            pltpu.VMEM((CLIPS, 2, 128), BF16),
            dma((9,)), dma, dma((2,)), dma, dma, dma, dma((CLIPS,)), dma, dma((2,)), pltpu.SemaphoreType.REGULAR((2,)),
            dma, dma((2,)), dma, dma((CHIPS,)), dma, dma((4,)), dma, dma((2,)),
        ],
        compiler_params=pltpu.CompilerParams(collective_id=0, has_side_effects=True),
        name="mlp",
    )(patches, frame_counts, patch_mask, norm_gain, up_weight, up_bias, down_weight.T, down_bias)


def solution(mesh):
    in_specs = (
        P("tok", "feat"), P("tok"), P("tok"), P("feat"), P("feat", "tok"), P("tok"), P("tok", "feat"), P("feat"),
    )
    return jax.shard_map(per_device, mesh=mesh, in_specs=in_specs, out_specs=P("tok", "feat"), check_vma=False)
```

```python
import functools
import math

import jax
import jax.numpy as jnp
from jax import lax
from jax.experimental import pallas as pl
from jax.experimental.pallas import tpu as pltpu
from jax.sharding import PartitionSpec as P

MESH = pl.DeviceIdType.MESH
BF16, F32 = jnp.bfloat16, jnp.float32
FRAME_TOK = 4
EPSILON = 1e-06
NZ, NX, NY = 16, 2, 8
CLIPS = NZ * NX
CHIPS = NY * 2
CHUNKS = 4
ROWS = 12
D_DEV = 192
FF_DEV = 768
HALF = FF_DEV // 2
OWN = 2 * ROWS
D_MODEL = 6144
CLOSE = [(step, flip) for step in (2, -2, 1, -1, 0) for flip in (1, 0) if step or flip]


def mod(a, n):
    return lax.rem(a + n, n)


def chip_peer(chip, k):
    y, column, i = lax.div(chip, 2), lax.rem(chip, 2), lax.div(k, 2)
    step = NY // 2 + lax.div(i + 1, 2) * (1 - 2 * lax.rem(i, 2))
    return mod(y + step, NY) * 2 + lax.rem(column + 1 + lax.rem(k, 2), 2)


def send(src, dst, send_sem, recv_sem, device):
    pltpu.make_async_remote_copy(
        src_ref=src, dst_ref=dst, send_sem=send_sem, recv_sem=recv_sem, device_id=device, device_id_type=MESH
    ).start()


def settle(ref, sem):
    pltpu.make_async_copy(ref, ref, sem).wait()


def gelu(v):
    return 0.5 * v * (1.0 + jnp.tanh(math.sqrt(2.0 / math.pi) * (v + 0.044715 * (v * v * v))))


def kernel(
    x_hbm, counts_hbm, mask_hbm, gain_hbm, w1_hbm, b1_hbm, w2_hbm, b2_hbm, out,
    xv, counts, mask, b1, b2, outv, xg, w1c, w2v, gains, gsend, grecv, stsend, strecv, turned, pbuf, precv, hid, qbuf, qrecv, qtail, qrtail,
    local, ws, wr, gs, gr, xs, xr, xfs, xfr, here, ps, pr, hs, hr, hfs, hfr, qs, qr,
):
    tok, feat = lax.axis_index("tok"), lax.axis_index("feat")
    z, column = lax.rem(tok, NZ), lax.div(tok, NZ)
    core, chip = lax.rem(feat, 2), lax.div(feat, 2)
    x, y = lax.rem(chip, 2) * 2 + column, lax.div(chip, 2)
    other = 1 - core
    partner = {"feat": feat + 1 - 2 * core}

    def local_copy(i, src, dst):
        copy = pltpu.make_async_copy(src, dst, local.at[i])
        copy.start()
        return copy

    x_in = local_copy(0, x_hbm, xv)
    gain_in = local_copy(1, gain_hbm, gains.at[core, 0])
    w1_in = local_copy(2, w1_hbm.at[:, pl.ds(pl.multiple_of(core * HALF, 128), HALF)], w1c.at[core])
    small_in = [local_copy(3 + i, *pair) for i, pair in enumerate(((b1_hbm, b1), (b2_hbm, b2), (counts_hbm, counts), (mask_hbm, mask)))]
    w2_in = local_copy(7, w2_hbm, w2v)

    def clip_at(step, c):
        return c * NZ + mod(z + step, NZ)

    def chip_at(step, flip):
        column2 = lax.rem(chip + flip, 2)
        return mod(y + step, NY) * 2 + column2

    barrier = pltpu.get_barrier_semaphore()

    def greet(device):
        pl.semaphore_signal(barrier, inc=1, device_id=device, device_id_type=MESH)

    steps = [d * sign for d in (4, 3, 2, 1) for sign in (1, -1)]
    for step in steps:
        for c in range(NX):
            greet({"tok": clip_at(step, c)})
    for step, flip in CLOSE:
        greet({"feat": chip_at(step, flip) * 2 + core})
    beside = (1 - column) * NZ + z
    greet({"tok": beside})
    greet(partner)

    x_in.wait()
    rows = xv[...].astype(F32)
    for i in range(3):
        xg[core, tok, i] = rows[4 * i : 4 * i + 4].astype(BF16)
    pl.semaphore_wait(barrier, 2 * len(steps) + len(CLOSE) + 2)

    def push(source, target):
        send(xg.at[core, source], xg.at[core, source], xs, xr.at[source], {"tok": target})

    def pass_on(source, far):
        send(xg.at[core, source], xg.at[core, source], xfs, xfr.at[far], partner)

    def arrive(source):
        settle(xg.at[core, source], xr.at[source])

    for step in steps:
        for c in range(NX):
            push(tok, clip_at(step, c))
    push(tok, beside)
    pass_on(tok, 0)
    send(w1_hbm.at[:, pl.ds(pl.multiple_of(other * HALF, 128), HALF)], w1c.at[core], ws, wr.at[0], partner)
    gain_in.wait()
    send(gains.at[core], gains.at[core], gs, wr.at[1], partner)
    for i, step in enumerate((-2, 2)):
        pl.semaphore_signal(here.at[1 - i], inc=1, device_id={"feat": chip_at(step, 0) * 2 + core}, device_id_type=MESH)

    for source in [beside] + [clip_at(sign * d, c) for d in (1, 2, 3) for sign in (1, -1) for c in range(NX)]:
        arrive(source)
        pass_on(source, 0)
    for c in range(NX):
        arrive(clip_at(-4, c))
        for step in (4, 3, 2, 1):
            push(clip_at(-4, c), clip_at(step, column))
    for c in range(NX):
        arrive(clip_at(4, c))
        for step in (-3, -2, -1):
            push(clip_at(4, c), clip_at(step, column))
    for c in range(NX):
        pass_on(clip_at(-4, c), lax.rem(z, 2))
        pass_on(clip_at(4, c), 1 - lax.rem(z, 2))

    for i in range(2):
        pl.semaphore_wait(here.at[i], 1)

    w1_in.wait()
    settle(w1c.at[0], wr.at[0])
    settle(gains.at[0], wr.at[1])
    total = jnp.zeros((1, HALF), F32)
    for h in range(2):
        part = gains[h]
        for _ in range(3):
            top = part.astype(BF16)
            total += jnp.dot(jnp.broadcast_to(top, (16, D_DEV)), w1c[h], preferred_element_type=F32)[0:1]
            part = part - top.astype(F32)
    gsend[...] = total

    @pl.loop(0, CHIPS - 1)
    def _(k):
        send(gsend, grecv.at[chip], gs, gr, {"feat": chip_peer(chip, k) * 2 + core})

    own_g = pltpu.make_async_copy(gsend, grecv.at[chip], gr)
    own_g.start()

    lane = lax.broadcasted_iota(jnp.int32, (4 * OWN, 128), 1)
    base = 2 * lax.div(z + 1, 2) - 4

    def first_product(far):
        settle(xg.at[0, pl.ds(0, CLIPS // 2)], xfr.at[far])

        @pl.loop(0, NX)
        def _(c):
            q = far * NX + c
            clips = [c * NZ + mod(base + 8 * far + i, NZ) for i in range(8)]
            rows = [
                jnp.concatenate([xg[h, clip, j].astype(F32) for clip in clips for j in range(3)], axis=0) for h in range(2)
            ]
            mean = sum(jnp.sum(r, axis=1, keepdims=True) for r in rows) * (1.0 / (2 * D_DEV))
            square = sum(jnp.sum(r * r, axis=1, keepdims=True) for r in rows)
            product = sum(
                jnp.dot(((rows[h] - mean) * gains[h]).astype(BF16), w1c[h], preferred_element_type=F32) for h in range(2)
            )
            owners = [(2 * i + far) * 2 + c for i in range(4)]
            for i, owner in enumerate(owners):
                pbuf[owner] = product[OWN * i : OWN * (i + 1)].astype(BF16)
            stat = jnp.where(lane == 0, mean, jnp.where(lane == 1, square, 0.0))
            stat = jnp.concatenate([stat, jnp.zeros((128 - 4 * OWN, 128), F32)], axis=0)
            stsend[q] = jnp.transpose(stat)[0:2]
            for owner in owners:

                @pl.when(owner != chip)
                def _():
                    send(pbuf.at[owner], precv.at[chip], ps, pr.at[0], {"feat": owner * 2 + core})
                    send(stsend.at[q], strecv.at[chip], ps, pr.at[1], {"feat": owner * 2 + core})

                @pl.when(owner == chip)
                def _():
                    pltpu.make_async_copy(pbuf.at[owner], precv.at[chip], pr.at[0]).start()
                    pltpu.make_async_copy(stsend.at[q], strecv.at[chip], pr.at[1]).start()

    first_product(0)
    for source in [clip_at(sign * d, c) for d in (5, 6, 7) for sign in (1, -1) for c in range(NX)] + [clip_at(8, c) for c in range(NX)]:
        arrive(source)
        pass_on(source, 1)

    first_product(1)
    settle(xg.at[0, pl.ds(0, CLIPS - 1)], xs)

    settle(grecv, gr)
    settle(strecv, pr.at[1])
    turned[0] = jnp.transpose(jnp.concatenate([strecv[:, 0, :], jnp.zeros((112, 128), F32)], axis=0))
    turned[1] = jnp.transpose(jnp.concatenate([strecv[:, 1, :], jnp.zeros((112, 128), F32)], axis=0))
    place = lax.div(y, 2)
    mine = pl.ds(pl.multiple_of(place * OWN, 8), OWN)
    means = turned[0, mine]
    mean = jnp.sum(means, axis=1, keepdims=True) * (1.0 / CHIPS)
    spread = jnp.sum(turned[1, mine], axis=1, keepdims=True) * (1.0 / D_MODEL) - mean * mean
    settle(precv, pr.at[0])
    acc = jnp.zeros((OWN, HALF), F32)
    for s in range(CHIPS):
        acc += precv[s].astype(F32) + (means[:, s : s + 1] - mean) * grecv[s]
    small_in[0].wait()
    bias = b1[pl.ds(pl.multiple_of(core * HALF, 128), HALF)].reshape(1, HALF)
    hid[core, chip] = gelu(acc * lax.rsqrt(spread + EPSILON) + bias).astype(BF16)

    def block_to(source, device_chip):
        send(hid.at[core, source], hid.at[core, source], hs, hr.at[source], {"feat": device_chip * 2 + core})

    for step, flip in CLOSE:
        block_to(chip, chip_at(step, flip))
    send(hid.at[core, chip], hid.at[core, chip], hfs, hfr.at[0], partner)

    places = (
        ((0, 0), (1, 0), (-1, 0), (0, 1)),
        ((2, 0), (-2, 0), (1, 1), (-1, 1)),
        ((2, 1), (-2, 1), (3, 0), (-3, 0)),
        ((4, 0), (3, 1), (-3, 1), (4, 1)),
    )
    groups = [[chip_at(*place) for place in group] for group in places]

    def collect(g, first, last):
        for place in places[g][first:last]:
            source = chip_at(*place)
            settle(hid.at[core, source], hr.at[source])
            for step in {-2: (1, 2), 2: (-1,)}.get(place[0], ()):
                block_to(source, chip_at(step, 0))
            send(hid.at[core, source], hid.at[core, source], hfs, hfr.at[g], partner)

    def second_product(g):
        settle(hid.at[0, pl.ds(0, 4)], hfr.at[g])
        rows = [jnp.concatenate([hid[h, owner].astype(F32) for owner in groups[g]], axis=0).astype(BF16) for h in range(2)]
        product = sum(
            lax.dot_general(
                rows[h], w2v[:, h * HALF : (h + 1) * HALF], (((1,), (1,)), ((), ())), preferred_element_type=F32
            )
            for h in range(2)
        )
        ahead = pltpu.roll(product[:, 128:], 4 * OWN - 6, 0)
        narrow = jnp.concatenate([product[:, 128:], ahead], axis=1)
        clips = []
        for owner in groups[g]:
            y2 = lax.div(owner, 2)
            first = base + 2 * lax.div(y2, 2) + 8 * lax.rem(y2, 2)
            clips += [lax.rem(owner, 2) * NZ + mod(first + e, NZ) for e in range(2)]
        for i, clip in enumerate(clips):
            packed = [product[ROWS * i : ROWS * (i + 1), :128], narrow[ROWS * i : ROWS * i + 4]]
            qbuf[clip] = jnp.concatenate(packed, axis=0).astype(BF16)
            qtail[clip] = narrow[ROWS * i + 4 : ROWS * i + 6].astype(BF16)
        for clip in clips:

            @pl.when(clip != tok)
            def _():
                send(qbuf.at[clip], qrecv.at[tok], qs, qr.at[0], {"tok": clip})
                send(qtail.at[clip], qrtail.at[tok], qs, qr.at[1], {"tok": clip})

            @pl.when(clip == tok)
            def _():
                pltpu.make_async_copy(qbuf.at[clip], qrecv.at[tok], qr.at[0]).start()
                pltpu.make_async_copy(qtail.at[clip], qrtail.at[tok], qr.at[1]).start()

    w2_in.wait()
    collect(0, 1, 4)
    collect(1, 0, 4)
    collect(2, 0, 2)
    second_product(0)
    second_product(1)
    collect(2, 2, 4)
    second_product(2)
    collect(3, 0, 4)
    second_product(3)

    for copy in small_in[1:]:
        copy.wait()
    position = lax.broadcasted_iota(jnp.int32, (ROWS, ROWS), 0)
    lane = lax.broadcasted_iota(jnp.int32, (ROWS, ROWS), 1)
    kept = jnp.where(position == lane, jnp.broadcast_to(mask[...].reshape(1, ROWS), (ROWS, ROWS)), 0)
    kept = jnp.sum(kept.astype(F32), axis=1, keepdims=True)
    present = jnp.broadcast_to(counts[...].reshape(1, 1), (ROWS, 1)) > lax.div(position[:, :1], FRAME_TOK)
    valid = jnp.where(present & (kept == 1.0), 1.0, 0.0)
    settle(qrtail, qr.at[1])
    settle(qrecv, qr.at[0])
    acc, tail = qrecv[0].astype(F32), qrtail[0].astype(F32)
    for s in range(1, CLIPS):
        acc += qrecv[s].astype(F32)
        tail += qrtail[s].astype(F32)
    acc = jnp.concatenate([acc, tail], axis=0)
    narrow = jnp.concatenate([acc[12:18, :64], acc[12:18, 64:]], axis=0)
    acc = jnp.concatenate([acc[:ROWS], narrow], axis=1)
    out[...] = (valid * (acc + b2[...].reshape(1, D_DEV))).astype(BF16)


    settle(w1c.at[0], ws)
    settle(gains.at[0], gs)
    settle(grecv.at[pl.ds(0, CHIPS - 1)], gs)
    settle(xg.at[0], xfs)
    settle(pbuf.at[pl.ds(0, CHIPS - 1)], ps)
    settle(strecv.at[pl.ds(0, CHIPS - 1)], ps)
    settle(hid.at[0, pl.ds(0, CHIPS - 1)], hs)
    settle(hid.at[0], hfs)
    settle(qbuf.at[pl.ds(0, CLIPS - 1)], qs)
    settle(qtail.at[pl.ds(0, CLIPS - 1)], qs)


def per_device(patches, frame_counts, patch_mask, norm_gain, up_weight, up_bias, down_weight, down_bias):
    hbm = pl.BlockSpec(memory_space=pltpu.HBM)
    dma = pltpu.SemaphoreType.DMA
    return pl.pallas_call(
        kernel,
        out_shape=pltpu.VMEM(patches.shape, BF16),
        in_specs=[hbm] * 8,
        out_specs=pl.BlockSpec(memory_space=pltpu.VMEM),
        scratch_shapes=[
            pltpu.VMEM((ROWS, D_DEV), BF16),
            pltpu.VMEM((1,), jnp.int32),
            pltpu.VMEM((ROWS,), jnp.int32),
            pltpu.VMEM((FF_DEV,), F32),
            pltpu.VMEM((D_DEV,), F32),
            pltpu.VMEM((ROWS, D_DEV), BF16),
            pltpu.VMEM((2, CLIPS, 3, 4, D_DEV), BF16),
            pltpu.VMEM((2, D_DEV, HALF), BF16),
            pltpu.VMEM((D_DEV, FF_DEV), BF16),
            pltpu.VMEM((2, 1, D_DEV), F32),
            pltpu.VMEM((1, HALF), F32),
            pltpu.VMEM((CHIPS, 1, HALF), F32),
            pltpu.VMEM((CHUNKS, 2, 128), F32),
            pltpu.VMEM((CHIPS, 2, 128), F32),
            pltpu.VMEM((2, 128, 128), F32),
            pltpu.VMEM((CHIPS, OWN, HALF), BF16),
            pltpu.VMEM((CHIPS, OWN, HALF), BF16),
            pltpu.VMEM((2, CHIPS, OWN, HALF), BF16),
            pltpu.VMEM((CLIPS, 16, 128), BF16),
            pltpu.VMEM((CLIPS, 16, 128), BF16),
            pltpu.VMEM((CLIPS, 2, 128), BF16),
            pltpu.VMEM((CLIPS, 2, 128), BF16),
            dma((9,)), dma, dma((2,)), dma, dma, dma, dma((CLIPS,)), dma, dma((2,)), pltpu.SemaphoreType.REGULAR((2,)),
            dma, dma((2,)), dma, dma((CHIPS,)), dma, dma((4,)), dma, dma((2,)),
        ],
        compiler_params=pltpu.CompilerParams(collective_id=0, has_side_effects=True),
        name="mlp",
    )(patches, frame_counts, patch_mask, norm_gain, up_weight, up_bias, down_weight.T, down_bias)


def solution(mesh):
    in_specs = (
        P("tok", "feat"), P("tok"), P("tok"), P("feat"), P("feat", "tok"), P("tok"), P("tok", "feat"), P("feat"),
    )
    return jax.shard_map(per_device, mesh=mesh, in_specs=in_specs, out_specs=P("tok", "feat"), check_vma=False)
```

```python
import functools
import math

import jax
import jax.numpy as jnp
from jax import lax
from jax.experimental import pallas as pl
from jax.experimental.pallas import tpu as pltpu
from jax.sharding import PartitionSpec as P

MESH = pl.DeviceIdType.MESH
BF16, F32 = jnp.bfloat16, jnp.float32
FRAME_TOK = 4
EPSILON = 1e-06
NZ, NX, NY = 16, 2, 8
CLIPS = NZ * NX
CHIPS = NY * 2
CHUNKS = 4
ROWS = 12
D_DEV = 192
FF_DEV = 768
HALF = FF_DEV // 2
OWN = 2 * ROWS
D_MODEL = 6144
CLOSE = [(step, flip) for step in (2, -2, 1, -1, 0) for flip in (1, 0) if step or flip]


def mod(a, n):
    return lax.rem(a + n, n)


def chip_peer(chip, k):
    y, column, i = lax.div(chip, 2), lax.rem(chip, 2), lax.div(k, 2)
    step = NY // 2 + lax.div(i + 1, 2) * (1 - 2 * lax.rem(i, 2))
    return mod(y + step, NY) * 2 + lax.rem(column + 1 + lax.rem(k, 2), 2)


def send(src, dst, send_sem, recv_sem, device):
    pltpu.make_async_remote_copy(
        src_ref=src, dst_ref=dst, send_sem=send_sem, recv_sem=recv_sem, device_id=device, device_id_type=MESH
    ).start()


def settle(ref, sem):
    pltpu.make_async_copy(ref, ref, sem).wait()


def gelu(v):
    return 0.5 * v * (1.0 + jnp.tanh(math.sqrt(2.0 / math.pi) * (v + 0.044715 * (v * v * v))))


def kernel(
    x_hbm, counts_hbm, mask_hbm, gain_hbm, w1_hbm, b1_hbm, w2_hbm, b2_hbm, out,
    xv, counts, mask, b1, b2, outv, xg, w1c, w2v, gains, gsend, grecv, stsend, strecv, turned, pbuf, precv, hid, qbuf, qrecv, qtail, qrtail,
    local, ws, wr, gs, gr, xs, xr, xfs, xfr, here, ps, pr, hs, hr, hfs, hfr, qs, qr,
):
    tok, feat = lax.axis_index("tok"), lax.axis_index("feat")
    z, column = lax.rem(tok, NZ), lax.div(tok, NZ)
    core, chip = lax.rem(feat, 2), lax.div(feat, 2)
    x, y = lax.rem(chip, 2) * 2 + column, lax.div(chip, 2)
    other = 1 - core
    partner = {"feat": feat + 1 - 2 * core}

    def local_copy(i, src, dst):
        copy = pltpu.make_async_copy(src, dst, local.at[i])
        copy.start()
        return copy

    def clip_at(step, c):
        return c * NZ + mod(z + step, NZ)

    def chip_at(step, flip):
        column2 = lax.rem(chip + flip, 2)
        return mod(y + step, NY) * 2 + column2

    barrier = pltpu.get_barrier_semaphore()

    def greet(device):
        pl.semaphore_signal(barrier, inc=1, device_id=device, device_id_type=MESH)

    steps = [d * sign for d in (4, 3, 2, 1) for sign in (1, -1)]
    for step in steps:
        for c in range(NX):
            greet({"tok": clip_at(step, c)})
    for step, flip in CLOSE:
        greet({"feat": chip_at(step, flip) * 2 + core})
    beside = (1 - column) * NZ + z
    greet({"tok": beside})
    greet(partner)

    x_in = local_copy(0, x_hbm, xv)
    gain_in = local_copy(1, gain_hbm, gains.at[core, 0])
    w1_in = local_copy(2, w1_hbm.at[:, pl.ds(pl.multiple_of(core * HALF, 128), HALF)], w1c.at[core])
    small_in = [local_copy(3 + i, *pair) for i, pair in enumerate(((b1_hbm, b1), (b2_hbm, b2), (counts_hbm, counts), (mask_hbm, mask)))]
    w2_in = local_copy(7, w2_hbm, w2v)

    x_in.wait()
    rows = xv[...].astype(F32)
    for i in range(3):
        xg[core, tok, i] = rows[4 * i : 4 * i + 4].astype(BF16)
    pl.semaphore_wait(barrier, 2 * len(steps) + len(CLOSE) + 2)

    def push(source, target):
        send(xg.at[core, source], xg.at[core, source], xs, xr.at[source], {"tok": target})

    def pass_on(source, far):
        send(xg.at[core, source], xg.at[core, source], xfs, xfr.at[far], partner)

    def arrive(source):
        settle(xg.at[core, source], xr.at[source])

    for step in steps:
        for c in range(NX):
            push(tok, clip_at(step, c))
    push(tok, beside)
    pass_on(tok, 0)
    send(w1_hbm.at[:, pl.ds(pl.multiple_of(other * HALF, 128), HALF)], w1c.at[core], ws, wr.at[0], partner)
    gain_in.wait()
    send(gains.at[core], gains.at[core], gs, wr.at[1], partner)
    for i, step in enumerate((-2, 2)):
        pl.semaphore_signal(here.at[1 - i], inc=1, device_id={"feat": chip_at(step, 0) * 2 + core}, device_id_type=MESH)

    for source in [beside] + [clip_at(sign * d, c) for d in (1, 2, 3) for sign in (1, -1) for c in range(NX)]:
        arrive(source)
        pass_on(source, 0)
    for c in range(NX):
        arrive(clip_at(-4, c))
        for step in (4, 3, 2, 1):
            push(clip_at(-4, c), clip_at(step, column))
    for c in range(NX):
        arrive(clip_at(4, c))
        for step in (-3, -2, -1):
            push(clip_at(4, c), clip_at(step, column))
    for c in range(NX):
        pass_on(clip_at(-4, c), lax.rem(z, 2))
        pass_on(clip_at(4, c), 1 - lax.rem(z, 2))

    for i in range(2):
        pl.semaphore_wait(here.at[i], 1)

    w1_in.wait()
    settle(w1c.at[0], wr.at[0])
    settle(gains.at[0], wr.at[1])
    total = jnp.zeros((1, HALF), F32)
    for h in range(2):
        part = gains[h]
        for _ in range(3):
            top = part.astype(BF16)
            total += jnp.dot(jnp.broadcast_to(top, (16, D_DEV)), w1c[h], preferred_element_type=F32)[0:1]
            part = part - top.astype(F32)
    gsend[...] = total

    @pl.loop(0, CHIPS - 1)
    def _(k):
        send(gsend, grecv.at[chip], gs, gr, {"feat": chip_peer(chip, k) * 2 + core})

    own_g = pltpu.make_async_copy(gsend, grecv.at[chip], gr)
    own_g.start()

    lane = lax.broadcasted_iota(jnp.int32, (4 * OWN, 128), 1)
    base = 2 * lax.div(z + 1, 2) - 4

    def first_product(far):
        settle(xg.at[0, pl.ds(0, CLIPS // 2)], xfr.at[far])

        @pl.loop(0, NX)
        def _(c):
            q = far * NX + c
            clips = [c * NZ + mod(base + 8 * far + i, NZ) for i in range(8)]
            rows = [
                jnp.concatenate([xg[h, clip, j].astype(F32) for clip in clips for j in range(3)], axis=0) for h in range(2)
            ]
            mean = sum(jnp.sum(r, axis=1, keepdims=True) for r in rows) * (1.0 / (2 * D_DEV))
            square = sum(jnp.sum(r * r, axis=1, keepdims=True) for r in rows)
            product = sum(
                jnp.dot(((rows[h] - mean) * gains[h]).astype(BF16), w1c[h], preferred_element_type=F32) for h in range(2)
            )
            owners = [(2 * i + far) * 2 + c for i in range(4)]
            for i, owner in enumerate(owners):
                pbuf[owner] = product[OWN * i : OWN * (i + 1)].astype(BF16)
            stat = jnp.where(lane == 0, mean, jnp.where(lane == 1, square, 0.0))
            stat = jnp.concatenate([stat, jnp.zeros((128 - 4 * OWN, 128), F32)], axis=0)
            stsend[q] = jnp.transpose(stat)[0:2]
            for owner in owners:

                @pl.when(owner != chip)
                def _():
                    send(pbuf.at[owner], precv.at[chip], ps, pr.at[0], {"feat": owner * 2 + core})
                    send(stsend.at[q], strecv.at[chip], ps, pr.at[1], {"feat": owner * 2 + core})

                @pl.when(owner == chip)
                def _():
                    pltpu.make_async_copy(pbuf.at[owner], precv.at[chip], pr.at[0]).start()
                    pltpu.make_async_copy(stsend.at[q], strecv.at[chip], pr.at[1]).start()

    first_product(0)
    for source in [clip_at(sign * d, c) for d in (5, 6, 7) for sign in (1, -1) for c in range(NX)] + [clip_at(8, c) for c in range(NX)]:
        arrive(source)
        pass_on(source, 1)

    first_product(1)
    settle(xg.at[0, pl.ds(0, CLIPS - 1)], xs)

    settle(grecv, gr)
    settle(strecv, pr.at[1])
    turned[0] = jnp.transpose(jnp.concatenate([strecv[:, 0, :], jnp.zeros((112, 128), F32)], axis=0))
    turned[1] = jnp.transpose(jnp.concatenate([strecv[:, 1, :], jnp.zeros((112, 128), F32)], axis=0))
    place = lax.div(y, 2)
    mine = pl.ds(pl.multiple_of(place * OWN, 8), OWN)
    means = turned[0, mine]
    mean = jnp.sum(means, axis=1, keepdims=True) * (1.0 / CHIPS)
    spread = jnp.sum(turned[1, mine], axis=1, keepdims=True) * (1.0 / D_MODEL) - mean * mean
    settle(precv, pr.at[0])
    acc = jnp.zeros((OWN, HALF), F32)
    for s in range(CHIPS):
        acc += precv[s].astype(F32) + (means[:, s : s + 1] - mean) * grecv[s]
    small_in[0].wait()
    bias = b1[pl.ds(pl.multiple_of(core * HALF, 128), HALF)].reshape(1, HALF)
    hid[core, chip] = gelu(acc * lax.rsqrt(spread + EPSILON) + bias).astype(BF16)

    def block_to(source, device_chip):
        send(hid.at[core, source], hid.at[core, source], hs, hr.at[source], {"feat": device_chip * 2 + core})

    for step, flip in CLOSE:
        block_to(chip, chip_at(step, flip))
    send(hid.at[core, chip], hid.at[core, chip], hfs, hfr.at[0], partner)

    places = (
        ((0, 0), (1, 0), (-1, 0), (0, 1)),
        ((2, 0), (-2, 0), (1, 1), (-1, 1)),
        ((2, 1), (-2, 1), (3, 0), (-3, 0)),
        ((4, 0), (3, 1), (-3, 1), (4, 1)),
    )
    groups = [[chip_at(*place) for place in group] for group in places]

    def collect(g, first, last):
        for place in places[g][first:last]:
            source = chip_at(*place)
            settle(hid.at[core, source], hr.at[source])
            for step in {-2: (1, 2), 2: (-1,)}.get(place[0], ()):
                block_to(source, chip_at(step, 0))
                if place[1]:
                    cross = {"feat": chip_at(step, 0) * 2 + other}
                    send(hid.at[core, source], hid.at[core, source], hfs, hfr.at[3], cross)
            if g < 3 or not place[1]:
                send(hid.at[core, source], hid.at[core, source], hfs, hfr.at[g], partner)

    def second_product(g):
        settle(hid.at[0, pl.ds(0, 4)], hfr.at[g])
        rows = [jnp.concatenate([hid[h, owner].astype(F32) for owner in groups[g]], axis=0).astype(BF16) for h in range(2)]
        product = sum(
            lax.dot_general(
                rows[h], w2v[:, h * HALF : (h + 1) * HALF], (((1,), (1,)), ((), ())), preferred_element_type=F32
            )
            for h in range(2)
        )
        ahead = pltpu.roll(product[:, 128:], 4 * OWN - 6, 0)
        narrow = jnp.concatenate([product[:, 128:], ahead], axis=1)
        clips = []
        for owner in groups[g]:
            y2 = lax.div(owner, 2)
            first = base + 2 * lax.div(y2, 2) + 8 * lax.rem(y2, 2)
            clips += [lax.rem(owner, 2) * NZ + mod(first + e, NZ) for e in range(2)]
        for i, clip in enumerate(clips):
            packed = [product[ROWS * i : ROWS * (i + 1), :128], narrow[ROWS * i : ROWS * i + 4]]
            qbuf[clip] = jnp.concatenate(packed, axis=0).astype(BF16)
            qtail[clip] = narrow[ROWS * i + 4 : ROWS * i + 6].astype(BF16)
        for clip in clips:

            @pl.when(clip != tok)
            def _():
                send(qbuf.at[clip], qrecv.at[tok], qs, qr.at[0], {"tok": clip})
                send(qtail.at[clip], qrtail.at[tok], qs, qr.at[1], {"tok": clip})

            @pl.when(clip == tok)
            def _():
                pltpu.make_async_copy(qbuf.at[clip], qrecv.at[tok], qr.at[0]).start()
                pltpu.make_async_copy(qtail.at[clip], qrtail.at[tok], qr.at[1]).start()

    w2_in.wait()
    collect(0, 1, 4)
    collect(1, 0, 4)
    collect(2, 0, 2)
    second_product(0)
    second_product(1)
    collect(2, 2, 4)
    second_product(2)
    collect(3, 0, 4)
    second_product(3)

    for copy in small_in[1:]:
        copy.wait()
    position = lax.broadcasted_iota(jnp.int32, (ROWS, ROWS), 0)
    lane = lax.broadcasted_iota(jnp.int32, (ROWS, ROWS), 1)
    kept = jnp.where(position == lane, jnp.broadcast_to(mask[...].reshape(1, ROWS), (ROWS, ROWS)), 0)
    kept = jnp.sum(kept.astype(F32), axis=1, keepdims=True)
    present = jnp.broadcast_to(counts[...].reshape(1, 1), (ROWS, 1)) > lax.div(position[:, :1], FRAME_TOK)
    valid = jnp.where(present & (kept == 1.0), 1.0, 0.0)
    settle(qrtail, qr.at[1])
    settle(qrecv, qr.at[0])
    acc, tail = qrecv[0].astype(F32), qrtail[0].astype(F32)
    for s in range(1, CLIPS):
        acc += qrecv[s].astype(F32)
        tail += qrtail[s].astype(F32)
    acc = jnp.concatenate([acc, tail], axis=0)
    narrow = jnp.concatenate([acc[12:18, :64], acc[12:18, 64:]], axis=0)
    acc = jnp.concatenate([acc[:ROWS], narrow], axis=1)
    out[...] = (valid * (acc + b2[...].reshape(1, D_DEV))).astype(BF16)


    settle(w1c.at[0], ws)
    settle(gains.at[0], gs)
    settle(grecv.at[pl.ds(0, CHIPS - 1)], gs)
    settle(xg.at[0], xfs)
    settle(pbuf.at[pl.ds(0, CHIPS - 1)], ps)
    settle(strecv.at[pl.ds(0, CHIPS - 1)], ps)
    settle(hid.at[0, pl.ds(0, CHIPS - 1)], hs)
    settle(hid.at[0], hfs)
    settle(qbuf.at[pl.ds(0, CLIPS - 1)], qs)
    settle(qtail.at[pl.ds(0, CLIPS - 1)], qs)


def per_device(patches, frame_counts, patch_mask, norm_gain, up_weight, up_bias, down_weight, down_bias):
    hbm = pl.BlockSpec(memory_space=pltpu.HBM)
    dma = pltpu.SemaphoreType.DMA
    return pl.pallas_call(
        kernel,
        out_shape=pltpu.VMEM(patches.shape, BF16),
        in_specs=[hbm] * 8,
        out_specs=pl.BlockSpec(memory_space=pltpu.VMEM),
        scratch_shapes=[
            pltpu.VMEM((ROWS, D_DEV), BF16),
            pltpu.VMEM((1,), jnp.int32),
            pltpu.VMEM((ROWS,), jnp.int32),
            pltpu.VMEM((FF_DEV,), F32),
            pltpu.VMEM((D_DEV,), F32),
            pltpu.VMEM((ROWS, D_DEV), BF16),
            pltpu.VMEM((2, CLIPS, 3, 4, D_DEV), BF16),
            pltpu.VMEM((2, D_DEV, HALF), BF16),
            pltpu.VMEM((D_DEV, FF_DEV), BF16),
            pltpu.VMEM((2, 1, D_DEV), F32),
            pltpu.VMEM((1, HALF), F32),
            pltpu.VMEM((CHIPS, 1, HALF), F32),
            pltpu.VMEM((CHUNKS, 2, 128), F32),
            pltpu.VMEM((CHIPS, 2, 128), F32),
            pltpu.VMEM((2, 128, 128), F32),
            pltpu.VMEM((CHIPS, OWN, HALF), BF16),
            pltpu.VMEM((CHIPS, OWN, HALF), BF16),
            pltpu.VMEM((2, CHIPS, OWN, HALF), BF16),
            pltpu.VMEM((CLIPS, 16, 128), BF16),
            pltpu.VMEM((CLIPS, 16, 128), BF16),
            pltpu.VMEM((CLIPS, 2, 128), BF16),
            pltpu.VMEM((CLIPS, 2, 128), BF16),
            dma((9,)), dma, dma((2,)), dma, dma, dma, dma((CLIPS,)), dma, dma((2,)), pltpu.SemaphoreType.REGULAR((2,)),
            dma, dma((2,)), dma, dma((CHIPS,)), dma, dma((4,)), dma, dma((2,)),
        ],
        compiler_params=pltpu.CompilerParams(collective_id=0, has_side_effects=True),
        name="mlp",
    )(patches, frame_counts, patch_mask, norm_gain, up_weight, up_bias, down_weight.T, down_bias)


def solution(mesh):
    in_specs = (
        P("tok", "feat"), P("tok"), P("tok"), P("feat"), P("feat", "tok"), P("tok"), P("tok", "feat"), P("feat"),
    )
    return jax.shard_map(per_device, mesh=mesh, in_specs=in_specs, out_specs=P("tok", "feat"), check_vma=False)
```
